256 devices in a mesh: dp: 32 (over y, x, core), tensor: 8 (over z).
Axes of the slice: x: 4, y: 4, z: 8, core: 2. Of those that a mesh axis runs over, the one named last changes fastest.
Arguments:
- activations: bfloat16 [2, 512, 8192], P(None, 'dp', 'tensor'), may hold values from -6 to 6
- gate_weight: bfloat16 [8192, 28672], P('tensor', 'dp'), may hold values from -0.0625 to 0.0625
- up_weight: bfloat16 [8192, 28672], P('tensor', 'dp'), may hold values from -0.0625 to 0.0625
- down_weight: bfloat16 [28672, 8192], P('dp', 'tensor'), may hold values from -0.03125 to 0.03125
- shrink_weight: bfloat16 [8192, 4096], P('tensor', 'dp'), may hold values from -0.0625 to 0.0625
- expand_weight: bfloat16 [2, 128, 16, 28672], P(None, 'tensor', None, 'dp'), may hold values from -1.5 to 1.5
- adapter_scale: float32 [128], P('dp'), may hold values from 0.5 to 2
- adapter_ids: int32 [512], replicated, may hold values from 0 to 127, as said below
Outputs:
- mixed: bfloat16 [2, 512, 8192], P(None, 'dp', 'tensor')
The draws below stay inside these ranges and needn't reach their ends.
Inputs may be any that keep to these rules, and one draw needn't show every extreme that they name: `adapter_ids`: at most 128 rows name adapters of one adapter block of 16 consecutive adapters, and in every draw some block is named by exactly 128 rows.
All inputs are finite; a program needn't handle non-finite values.
Results may differ from the reference program's by a relative error of at most 0.03.
Values may be sent and summed in bfloat16 or wider, within the bound.
A program may use at most 64 MiB of HBM per device.

```python
import math
import jax
import jax.numpy as jnp
from jax import lax

D = 8192
FF = 28672
R = 16
STEPS = 2
ROWS = 512
ADAPTERS = 128
ADP_T = 16
CAP_T = 128
N_TENSOR = 8


def draw_adapter_ids(key, part):
    key_hot, key_order, key_slots, key_local = jax.random.split(key, 4)
    blocks = ADAPTERS // ADP_T
    hot_block = jax.random.randint(key_hot, (), 0, blocks)
    position = jax.random.permutation(key_order, ROWS)
    slot_order = jax.random.permutation(key_slots, (blocks - 1) * CAP_T)
    slot_taken = slot_order[jnp.clip(position - CAP_T, 0, (blocks - 1) * CAP_T - 1)]
    other_block = slot_taken // CAP_T
    other_block = other_block + (other_block >= hot_block).astype(jnp.int32)
    chosen = jnp.where(position < CAP_T, hot_block, other_block)
    local_ids = jax.random.randint(key_local, (ROWS,), 0, ADP_T)
    return (chosen * ADP_T + local_ids).astype(jnp.int32)


def block_scale(rng, shape, cuts, least, top_value):
    loudness = 1.0
    for dim, blocks in cuts:
        draws = jax.random.uniform(jax.random.fold_in(jax.random.fold_in(rng, 6), dim), (blocks,), jnp.float32, least / len(cuts), top_value / len(cuts))
        loudness = loudness * jnp.repeat(jnp.exp(draws), shape[dim] // blocks).reshape((-1,) + (1,) * (len(shape) - 1 - dim))
    return loudness


def gaussian(own_key, dims, scale, limit, shards=(), kind=jnp.bfloat16):
    array = scale * jax.random.normal(own_key, dims, jnp.float32)
    if shards:
        array = array * block_scale(own_key, dims, shards, -0.22, 0.18)
    return jnp.clip(array, -limit, limit).astype(kind)


def setup_inputs(seed: int = 0) -> dict:
    arg_keys = jax.random.split(jax.random.key(seed), 9)
    return {
        "activations": gaussian(arg_keys[0], (STEPS, ROWS, D), 1.0, 6.0, ((1, 32), (2, 8))),
        "gate_weight": gaussian(arg_keys[1], (D, FF), D ** -0.5, 0.0625, ((0, 8), (1, 32))),
        "up_weight": gaussian(arg_keys[2], (D, FF), D ** -0.5, 0.0625, ((0, 8), (1, 32))),
        "down_weight": gaussian(arg_keys[3], (FF, D), FF ** -0.5, 0.03125, ((0, 32), (1, 8))),
        "shrink_weight": gaussian(arg_keys[4], (D, ADAPTERS * 2 * R), D ** -0.5, 0.0625, ((0, 8), (1, 32))),
        "expand_weight": gaussian(arg_keys[5], (2, ADAPTERS, R, FF), R ** -0.5, 1.5, ((1, 8), (3, 32))),
        "adapter_scale": jnp.clip(jnp.exp(math.log(2.0) - 1.3862944 * jax.random.uniform(arg_keys[6], (ADAPTERS,), jnp.float32) ** block_scale(arg_keys[6], (ADAPTERS,), ((0, 32),), -0.2, 0.2)), 0.5, 2.0),
        "adapter_ids": draw_adapter_ids(jax.random.fold_in(arg_keys[8], 71), 0),
    }


def reference(activations, gate_weight, up_weight, down_weight, shrink_weight, expand_weight, adapter_scale, adapter_ids):
    feat_width = D // N_TENSOR
    offsets = jnp.arange(ADP_T, dtype=jnp.int32)
    results = []
    for step_index in range(STEPS):
        tokens_now = activations[step_index]
        shrunk = jnp.dot(tokens_now, shrink_weight, preferred_element_type=jnp.float32).reshape(ROWS, ADAPTERS, 2 * R)
        picked = jnp.take_along_axis(shrunk, adapter_ids.astype(jnp.int32)[:, None, None], axis=1)[:, 0, :]
        low_inputs = (picked * adapter_scale[adapter_ids][:, None]).astype(jnp.bfloat16)
        gate_sum = jnp.zeros((ROWS, FF), jnp.float32)
        up_sum = jnp.zeros((ROWS, FF), jnp.float32)
        for block_index in range(N_TENSOR):
            member = (adapter_ids[:, None] == block_index * ADP_T + offsets[None, :]).astype(jnp.bfloat16)
            spread = jnp.repeat(member, R, axis=1)
            gate_low = jnp.tile(low_inputs[:, :R], (1, ADP_T)) * spread
            up_low = jnp.tile(low_inputs[:, R:], (1, ADP_T)) * spread
            first = block_index * feat_width
            slice_cols = tokens_now[:, first:first + feat_width]
            gate_expand = expand_weight[0, block_index * ADP_T:(block_index + 1) * ADP_T].reshape(ADP_T * R, FF)
            up_expand = expand_weight[1, block_index * ADP_T:(block_index + 1) * ADP_T].reshape(ADP_T * R, FF)
            gate_part = jnp.dot(slice_cols, gate_weight[first:first + feat_width], preferred_element_type=jnp.float32)
            gate_part = gate_part + jnp.dot(gate_low, gate_expand, preferred_element_type=jnp.float32)
            up_part = jnp.dot(slice_cols, up_weight[first:first + feat_width], preferred_element_type=jnp.float32)
            up_part = up_part + jnp.dot(up_low, up_expand, preferred_element_type=jnp.float32)
            gate_sum = gate_sum + lax.optimization_barrier(gate_part.astype(jnp.bfloat16)).astype(jnp.float32)
            up_sum = up_sum + lax.optimization_barrier(up_part.astype(jnp.bfloat16)).astype(jnp.float32)
        hidden = (jax.nn.silu(gate_sum) * up_sum).astype(jnp.bfloat16)
        results.append(jnp.dot(hidden, down_weight, preferred_element_type=jnp.float32).astype(jnp.bfloat16))
    return jnp.stack(results)
```

```python
import functools

import jax
import jax.numpy as jnp
from jax import lax
from jax.experimental import pallas as pl
from jax.experimental.pallas import tpu as pltpu

MESH = pl.DeviceIdType.MESH
BF = jnp.bfloat16
F32 = jnp.float32


def dot(a, b):
    return jnp.dot(a, b, preferred_element_type=F32)


def dot0(a, b):
    return lax.dot_general(a, b, (((0,), (0,)), ((), ())), preferred_element_type=F32)


def iota(shape, dim):
    return lax.broadcasted_iota(jnp.int32, shape, dim)


def layer_kernel(
    nx,
    ny,
    nz,
    x_hbm,
    wg_hbm,
    wu_hbm,
    wd_hbm,
    ws_hbm,
    we_hbm,
    scale_ref,
    ids_ref,
    out_ref,
    xg,
    wg,
    wu,
    wd,
    ws,
    we,
    idm,
    psrc,
    pdst,
    masked,
    lsend,
    lrecv,
    lbc,
    lowx,
    pg,
    pu,
    rg,
    ru,
    hid,
    dbuf,
    sbuf,
    rsb,
    own,
    wsem,
    lsem,
    ag1_s,
    ag1_r,
    ag2_s,
    ag2_r,
    sib_s,
    sib_r,
    lz_s,
    lz_r,
    lb_s,
    lb_r,
    lbs_s,
    lbs_r,
    rz_s,
    rz_r,
    az_s,
    az_r,
    sr_s,
    sr_r,
    rs_s,
    rs_r,
):
    nchip = nx * ny
    steps, rows, feat = x_hbm.shape
    half = xg.shape[2] // 2
    dp = lax.axis_index("dp")
    t = lax.axis_index("tensor")
    c = dp % 2
    chip = dp // 2
    x = chip % nx
    y = chip // nx
    m = (x + y) % nx
    pos = (y * 2 + c) * rows

    loads = [
        pltpu.make_async_copy(ws_hbm, ws, wsem.at[0]),
        pltpu.make_async_copy(wg_hbm, wg, wsem.at[1]),
        pltpu.make_async_copy(wu_hbm, wu, wsem.at[2]),
        pltpu.make_async_copy(we_hbm, we, wsem.at[3]),
        pltpu.make_async_copy(wd_hbm, wd, wsem.at[4]),
    ]
    mine = pltpu.make_async_copy(x_hbm, xg.at[:, m, pl.ds(pos, rows), :], lsem.at[0])
    mine.start()
    for load in loads:
        load.start()

    def peer(chip_to):
        return {"dp": chip_to * 2 + c, "tensor": t}

    sibling = {"dp": chip * 2 + 1 - c, "tensor": t}

    def plane(z):
        return {"dp": dp, "tensor": z % nz}

    barrier = pltpu.get_barrier_semaphore()
    for rel in range(1, nchip):
        pl.semaphore_signal(
            barrier, inc=1, device_id=peer((chip + rel) % nchip), device_id_type=MESH
        )
    pl.semaphore_signal(barrier, inc=1, device_id=sibling, device_id_type=MESH)
    for rel in range(1, nz):
        pl.semaphore_signal(barrier, inc=1, device_id=plane(t + rel), device_id_type=MESH)
    pl.semaphore_wait(barrier, nchip - 1 + 1 + nz - 1)

    def send(src, dst, ssem, rsem, dev):
        return pltpu.make_async_remote_copy(
            src_ref=src,
            dst_ref=dst,
            send_sem=ssem,
            recv_sem=rsem,
            device_id=dev,
            device_id_type=MESH,
        )

    na = nx
    a = x * (1 - c) + y * c
    b = y * (1 - c) + x * c

    def chip_at(ca, cb):
        cx = ca * (1 - c) + cb * c
        cy = ca * c + cb * (1 - c)
        return cy * nx + cx

    def block_at(ch, core):
        cx = ch % nx
        cy = ch // nx
        return xg.at[:, (cx + cy) % nx, pl.ds((cy * 2 + core) * rows, rows), :]

    def block_rel(d, e):
        return block_at(chip_at((a + na - d) % na, (b + na - e) % na), c)

    waits = []
    here = block_at(chip, c)
    for d in (1, 3, 2):
        cp = send(x_hbm, here, ag1_s.at[d - 1], ag1_r.at[d - 1], peer(chip_at((a + d) % na, b)))
        cp.start()
        waits.append(cp)
    for e in (1, 3, 2):
        cp = send(x_hbm, here, ag2_s.at[0, e - 1], ag2_r.at[0, e - 1], peer(chip_at(a, (b + e) % na)))
        cp.start()
        waits.append(cp)
    cp = send(x_hbm, here, sib_s.at[0, 0], sib_r.at[0, 0], sibling)
    cp.start()
    waits.append(cp)
    for d in (1, 3, 2):
        blk = block_rel(d, 0)
        send(blk, blk, ag1_s.at[d - 1], ag1_r.at[d - 1], sibling).wait_recv()
        for e in (1, 3, 2):
            cp = send(blk, blk, ag2_s.at[d, e - 1], ag2_r.at[d, e - 1], peer(chip_at(a, (b + e) % na)))
            cp.start()
            waits.append(cp)
        cp = send(blk, blk, sib_s.at[d, 0], sib_r.at[d, 0], sibling)
        cp.start()
        waits.append(cp)

    nrow = idm.shape[0]
    eye = iota((128, 128), 0) == iota((128, 128), 1)
    ones = jnp.ones((128, 128), BF)
    per = 128 // rows
    for q in range(nrow // 128):
        line = jnp.broadcast_to(ids_ref[pl.ds(q, 1), :], (128, 128))
        diag = jnp.where(eye, line, 0).astype(F32).astype(BF)
        col = dot(diag, ones).astype(jnp.int32)
        for i in range(per):
            g = q * per + i
            gc, gx, gy = g % 2, (g // 2) % nx, g // 2 // nx
            at = ((gx + gy) % nx) * 128 + (gy * 2 + gc) * rows
            idm[pl.ds(at, rows), :] = col[i * rows : (i + 1) * rows, :]
    ids = idm[...]
    lane = iota((nrow, 128), 1)
    tri = (iota((nrow, nrow), 1) < iota((nrow, nrow), 0)).astype(F32).astype(BF)
    jb = dp // 4
    for blk_id, ref in ((jb, psrc), (t, pdst)):
        member = (ids // 16) == blk_id
        rank = dot(tri, member.astype(F32).astype(BF)).astype(jnp.int32)
        ref[...] = jnp.where(member & (rank == lane), 1.0, 0.0).astype(BF)

    for d in range(na):
        for e in (1, 3, 2):
            blk = block_rel(d, e)
            send(blk, blk, ag2_s.at[d, e - 1], ag2_r.at[d, e - 1], sibling).wait_recv()
            cp = send(blk, blk, sib_s.at[d, e], sib_r.at[d, e], sibling)
            cp.start()
            waits.append(cp)
    mine.wait()
    loads[0].wait()
    for d in range(na):
        for e in range(na):
            blk = block_at(chip_at((a + na - e) % na, (b + na - d) % na), 1 - c)
            send(blk, blk, sib_s.at[d, e], sib_r.at[d, e], sibling).wait_recv()

    lane1 = iota((1, 128), 1)
    scale = jnp.where(
        lane1 < 64,
        jnp.where(lane1 < 32, scale_ref[0], scale_ref[1]),
        jnp.where(lane1 < 96, scale_ref[2], scale_ref[3]),
    )
    nm = xg.shape[1]

    def shrink(i, _):
        s, mm = i // nm, i % nm
        shr = dot(xg[s, mm], ws[...])
        keep = idm[pl.ds(pl.multiple_of(mm * 128, 128), 128), :] == dp * 4 + lane1 // 32
        masked[s, pl.ds(pl.multiple_of(mm * 128, 128), 128), :] = jnp.where(
            keep, shr * scale, 0.0
        ).astype(BF)
        return 0

    lax.fori_loop(0, steps * nm, shrink, 0)
    packed = jnp.zeros((64, 128), F32)
    fr, fc = iota((128, 128), 0), iota((128, 128), 1)
    for s in range(steps):
        comp = dot0(psrc[...], masked[s]).astype(BF)
        for h in range(2):
            q = 2 * s + h
            fold = ((fr % 32 == fc % 32) & (fc // 32 == q)).astype(F32).astype(BF)
            packed = packed + dot(comp[64 * h : 64 * h + 64], fold)
    lsend[...] = packed.astype(BF)
    root = t == jb
    rel = (t + nz - jb) % nz

    @pl.when(jnp.logical_not(root))
    def _():
        cp = send(lsend, lrecv.at[rel - 1], lz_s.at[0], lz_r.at[rel - 1], {"dp": dp, "tensor": jb})
        cp.start()

    @pl.when(root)
    def _():
        total = lsend[...].astype(F32)
        for r in range(nz - 1):
            send(lsend, lrecv.at[r], lz_s.at[0], lz_r.at[r], sibling).wait_recv()
            total = total + lrecv[r].astype(F32)
        lbc[dp % 4] = total.astype(BF)
        for r in range(1, nchip):
            send(
                lbc.at[dp % 4],
                lbc.at[dp % 4],
                lb_s.at[r - 1],
                lb_r.at[x % 2],
                peer((chip + r) % nchip),
            ).start()

    root_chip = t * 2
    for xi in range(2):
        slot = xi * 2 + c

        @pl.when(chip != root_chip + xi)
        def _():
            send(lbc.at[slot], lbc.at[slot], lb_s.at[0], lb_r.at[xi], sibling).wait_recv()

        cp = send(lbc.at[slot], lbc.at[slot], lbs_s.at[xi], lbs_r.at[xi], sibling)
        cp.start()
        waits.append(cp)
    for xi in range(2):
        slot = xi * 2 + 1 - c
        send(lbc.at[slot], lbc.at[slot], lbs_s.at[xi], lbs_r.at[xi], sibling).wait_recv()

    low = (
        lbc[0].astype(F32) + lbc[1].astype(F32) + lbc[2].astype(F32) + lbc[3].astype(F32)
    ).astype(BF)
    tr, tc = iota((128, 256), 0), iota((128, 256), 1)
    for s in range(steps):
        for u in range(2):
            parts = []
            for h in range(2):
                q = 2 * s + h
                spread = (tr == 32 * q + 16 * u + tc % 16).astype(F32).astype(BF)
                parts.append(dot(low[:, :], spread).astype(BF))
            tiled = jnp.concatenate(parts, axis=0)
            for w in range(2):
                wide = dot(pdst[...], tiled[:, w * 128 : w * 128 + 128])
                keep = idm[...] == t * 16 + w * 8 + lane // 16
                wide = jnp.where(keep, wide, 0.0).astype(BF)
                for mm in range(nm):
                    lowx[u, s * nm + mm, :, pl.ds(w * 128, 128)] = wide[mm * 128 : mm * 128 + 128]

    for load in loads[1:4]:
        load.wait()

    def partials(k):
        sg = (t + nz - 1 - k) % nz
        su = (t + 1 + k) % nz
        pg[...] = dot(xg[sg // nm, sg % nm], wg[...]) + dot(lowx[0, sg], we[0])
        pu[...] = dot(xg[su // nm, su % nm], wu[...]) + dot(lowx[1, su], we[1])

    def ring_copy(k, u, h):
        buf = ru if u else rg
        part = pl.ds(h * half, half)
        return send(
            buf.at[k, part],
            buf.at[k + 1, part],
            rz_s.at[u, h, k],
            rz_r.at[u, h, k],
            plane(t + (nz - 1 if u else 1)),
        )

    def ring(k, _):
        partials(k)
        for h in range(2):
            for u in range(2):
                buf, add = (ru, pu) if u else (rg, pg)
                part = pl.ds(h * half, half)

                @pl.when(k > 0)
                def _():
                    ring_copy(k - 1, u, h).wait_recv()
                    buf[k, part] = (buf[k, part].astype(F32) + add[part]).astype(BF)

                @pl.when(k == 0)
                def _():
                    buf[k, part] = add[part].astype(BF)

                ring_copy(k, u, h).start()
        return 0

    lax.fori_loop(0, nz - 1, ring, 0)
    partials(nz - 1)

    def gather_copy(v, d, h):
        shard = (t + nz - d) % nz if v == 0 else (t + d) % nz
        ref = hid.at[shard, pl.ds(h * half, half)]
        return send(
            ref, ref, az_s.at[v, h, d], az_r.at[v, h, d], plane(t + (1 if v == 0 else nz - 1))
        )

    for h in range(2):
        part = pl.ds(h * half, half)
        for u in range(2):
            ring_copy(nz - 2, u, h).wait_recv()
        gate = rg[nz - 1, part].astype(F32) + pg[part]
        up = ru[nz - 1, part].astype(F32) + pu[part]
        hid[t, part] = (gate / (1.0 + jnp.exp(-gate)) * up).astype(BF)
        for v in range(2):
            cp = gather_copy(v, 0, h)
            cp.start()
            waits.append(cp)
    loads[4].wait()

    far = nz // 2

    def down(shard, n):
        val = dot(hid[shard], wd[...]).astype(BF)
        for r in range(2 * ny):
            dbuf[n, r % 2, r // 2] = val[r * rows : (r + 1) * rows]
        cp = send(dbuf.at[n, 1 - c], sbuf.at[n], sr_s.at[n], sr_r.at[n], sibling)
        cp.start()
        waits.append(cp)

    def home_chip(shard, yy):
        mm = shard % nm
        return yy * nx + (mm + nx - yy) % nx

    def scatter_copy(shard, n, yy):
        hc = home_chip(shard, yy)
        rel = (chip + nchip - hc) % nchip
        s = shard // nm
        return send(
            dbuf.at[n, c, yy],
            rsb.at[s, rel - 1],
            rs_s.at[n, yy],
            rs_r.at[s, rel - 1],
            peer(hc),
        )

    def scatter(shard, n):
        send(dbuf.at[n, c], sbuf.at[n], sr_s.at[n], sr_r.at[n], sibling).wait_recv()
        for yy in range(ny):
            total = dbuf[n, c, yy].astype(F32) + sbuf[n, yy].astype(F32)
            at_home = home_chip(shard, yy) == chip

            @pl.when(at_home)
            def _():
                own[shard // nm] = total

            @pl.when(jnp.logical_not(at_home))
            def _():
                dbuf[n, c, yy] = total.astype(BF)
                scatter_copy(shard, n, yy).start()

    down(t, 0)
    pending = [(t, 0)]
    n = 1
    for d in range(1, far + 1):
        for h in range(2):
            for v in range(2):
                if d == far and v != h:
                    continue
                shard = (t + nz - d) % nz if v == 0 else (t + d) % nz
                ref = hid.at[shard, pl.ds(h * half, half)]
                send(ref, ref, az_s.at[v, h, d - 1], az_r.at[v, h, d - 1], sibling).wait_recv()
                if d < far - 1 or (d == far - 1 and v == h):
                    cp = gather_copy(v, d, h)
                    cp.start()
                    waits.append(cp)
        if d < far:
            todo = [(t + nz - d) % nz, (t + d) % nz]
        else:
            todo = [(t + far) % nz]
        for shard in todo:
            down(shard, n)
            pending.append((shard, n))
            scatter(*pending[n - 1])
            n += 1
    scatter(*pending[-1])

    for s in range(steps):
        total = own[s]
        for r in range(nchip - 1):
            send(rsb.at[s, r], rsb.at[s, r], rs_s.at[0, 0], rs_r.at[s, r], sibling).wait_recv()
            total = total + rsb[s, r].astype(F32)
        out_ref[s] = total.astype(BF)

    for cp in waits:
        cp.wait_send()
    for k in range(nz - 1):
        for h in range(2):
            for u in range(2):
                ring_copy(k, u, h).wait_send()

    @pl.when(jnp.logical_not(root))
    def _():
        send(lsend, lrecv.at[0], lz_s.at[0], lz_r.at[0], sibling).wait_send()

    @pl.when(root)
    def _():
        for r in range(1, nchip):
            send(lbc.at[0], lbc.at[0], lb_s.at[r - 1], lb_r.at[0], sibling).wait_send()

    for shard, i in pending:
        for yy in range(ny):

            @pl.when(home_chip(shard, yy) != chip)
            def _():
                scatter_copy(shard, i, yy).wait_send()


def per_device(nx, ny, nz, act, wg, wu, wd, ws, we, scale, ids):
    steps, rows, feat = act.shape
    ff = wg.shape[1]
    dout = wd.shape[1]
    nrow = ids.shape[0]
    nm = nx
    nchip = nx * ny
    we = we.reshape(2, we.shape[1] * we.shape[2], ff)
    ids2 = ids.reshape(nrow // 128, 128)
    dma = pltpu.SemaphoreType.DMA
    nshard = steps * nm
    anyspec = pl.BlockSpec(memory_space=pl.ANY)
    vmem = pl.BlockSpec(memory_space=pltpu.VMEM)
    return pl.pallas_call(
        functools.partial(layer_kernel, nx, ny, nz),
        out_shape=jax.ShapeDtypeStruct((steps, rows, dout), BF),
        in_specs=[anyspec] * 6 + [pl.BlockSpec(memory_space=pltpu.SMEM), vmem],
        out_specs=vmem,
        scratch_shapes=[
            pltpu.VMEM((steps, nm, 128, feat), BF),
            pltpu.VMEM(wg.shape, BF),
            pltpu.VMEM(wu.shape, BF),
            pltpu.VMEM(wd.shape, BF),
            pltpu.VMEM(ws.shape, BF),
            pltpu.VMEM(we.shape, BF),
            pltpu.VMEM((nrow, 128), jnp.int32),
            pltpu.VMEM((nrow, 128), BF),
            pltpu.VMEM((nrow, 128), BF),
            pltpu.VMEM((steps, nrow, 128), BF),
            pltpu.VMEM((64, 128), BF),
            pltpu.VMEM((nz - 1, 64, 128), BF),
            pltpu.VMEM((4, 64, 128), BF),
            pltpu.VMEM((2, nshard, 128, 256), BF),
            pltpu.VMEM((128, ff), F32),
            pltpu.VMEM((128, ff), F32),
            pltpu.VMEM((nz, 128, ff), BF),
            pltpu.VMEM((nz, 128, ff), BF),
            pltpu.VMEM((nz, 128, ff), BF),
            pltpu.VMEM((nshard, 2, ny, rows, dout), BF),
            pltpu.VMEM((nshard, ny, rows, dout), BF),
            pltpu.VMEM((steps, nchip - 1, rows, dout), BF),
            pltpu.VMEM((steps, rows, dout), F32),
            dma((5,)),
            dma((1,)),
            dma((3,)),
            dma((3,)),
            dma((4, 3)),
            dma((4, 3)),
            dma((4, 4)),
            dma((4, 4)),
            dma((1,)),
            dma((nz - 1,)),
            dma((nchip - 1,)),
            dma((2,)),
            dma((2,)),
            dma((2,)),
            dma((2, 2, nz - 1)),
            dma((2, 2, nz - 1)),
            dma((2, 2, 4)),
            dma((2, 2, 4)),
            dma((nshard,)),
            dma((nshard,)),
            dma((nshard, ny)),
            dma((steps, nchip - 1)),
        ],
        compiler_params=pltpu.CompilerParams(
            collective_id=0, has_side_effects=True, vmem_limit_bytes=60 * 1024 * 1024
        ),
        name="layer",
    )(act, wg, wu, wd, ws, we, scale, ids2)


def solution(mesh):
    placed = (
        jax.sharding.PartitionSpec(None, "dp", "tensor"),
        jax.sharding.PartitionSpec("tensor", "dp"),
        jax.sharding.PartitionSpec("tensor", "dp"),
        jax.sharding.PartitionSpec("dp", "tensor"),
        jax.sharding.PartitionSpec("tensor", "dp"),
        jax.sharding.PartitionSpec(None, "tensor", None, "dp"),
        jax.sharding.PartitionSpec("dp"),
        jax.sharding.PartitionSpec(),
    )
    return jax.shard_map(
        functools.partial(per_device, 4, 4, mesh.shape["tensor"]),
        mesh=mesh,
        in_specs=placed,
        out_specs=jax.sharding.PartitionSpec(None, "dp", "tensor"),
        check_vma=False,
    )
```

```python
import functools

import jax
import jax.numpy as jnp
from jax import lax
from jax.experimental import pallas as pl
from jax.experimental.pallas import tpu as pltpu

MESH = pl.DeviceIdType.MESH
BF = jnp.bfloat16
F32 = jnp.float32


def dot(a, b):
    return jnp.dot(a, b, preferred_element_type=F32)


def dot0(a, b):
    return lax.dot_general(a, b, (((0,), (0,)), ((), ())), preferred_element_type=F32)


def iota(shape, dim):
    return lax.broadcasted_iota(jnp.int32, shape, dim)


def layer_kernel(
    nx,
    ny,
    nz,
    x_hbm,
    wg_hbm,
    wu_hbm,
    wd_hbm,
    ws_hbm,
    we_hbm,
    scale_ref,
    ids_ref,
    out_ref,
    xg,
    wg,
    wu,
    wd,
    ws,
    scl,
    we,
    idm,
    psrc,
    pdst,
    masked,
    lsend,
    lrecv,
    lbc,
    low,
    lowx,
    pg,
    pu,
    rg,
    ru,
    hid,
    dbuf,
    sbuf,
    rsb,
    own,
    wsem,
    lsem,
    ag1_s,
    ag1_r,
    ag2_s,
    ag2_r,
    sib_s,
    sib_r,
    sw_s,
    sw_r,
    lz_s,
    lz_r,
    lb_s,
    lb_r,
    lbs_s,
    lbs_r,
    rz_s,
    rz_r,
    az_s,
    az_r,
    sr_s,
    sr_r,
    rs_s,
    rs_r,
):
    nchip = nx * ny
    steps, rows, feat = x_hbm.shape
    pairs = nchip // 2
    unit = 2 * rows
    span = steps * unit
    dp = lax.axis_index("dp")
    t = lax.axis_index("tensor")
    c = dp % 2
    chip = dp // 2
    x = chip % nx
    y = chip // nx

    def shard_of(ch, core, s):
        return (ch % pairs + 2 * pairs - 2 * core - pairs // 2 * s) % pairs

    def rows_of(ch, core, s, h):
        at = (2 * h + s) * unit + ch // pairs * rows
        return xg.at[shard_of(ch, core, s), pl.ds(at, rows), :]

    mine = [
        pltpu.make_async_copy(x_hbm.at[s], rows_of(chip, c, s, 0), lsem.at[s])
        for s in range(steps)
    ]
    loads = [
        pltpu.make_async_copy(ws_hbm, ws.at[c], wsem.at[0]),
        pltpu.make_async_copy(wg_hbm, wg, wsem.at[1]),
        pltpu.make_async_copy(wu_hbm, wu, wsem.at[2]),
        pltpu.make_async_copy(we_hbm, we, wsem.at[3]),
        pltpu.make_async_copy(wd_hbm, wd, wsem.at[4]),
    ]
    for load in mine + loads:
        load.start()

    def peer(chip_to):
        return {"dp": chip_to * 2 + c, "tensor": t}

    sibling = {"dp": chip * 2 + 1 - c, "tensor": t}

    def plane(z):
        return {"dp": dp, "tensor": z % nz}

    barrier = pltpu.get_barrier_semaphore()
    for rel in range(1, nchip):
        pl.semaphore_signal(
            barrier, inc=1, device_id=peer((chip + rel) % nchip), device_id_type=MESH
        )
    pl.semaphore_signal(barrier, inc=1, device_id=sibling, device_id_type=MESH)
    for rel in range(1, nz):
        pl.semaphore_signal(barrier, inc=1, device_id=plane(t + rel), device_id_type=MESH)

    eye = iota((128, 128), 0) == iota((128, 128), 1)
    ones = jnp.ones((128, 128), BF)
    per = 128 // rows
    nlow = idm.shape[2]
    for q in range(ids_ref.shape[0]):
        line = jnp.broadcast_to(ids_ref[pl.ds(q, 1), :], (128, 128))
        diag = jnp.where(eye, line, 0).astype(F32).astype(BF)
        col = dot(diag, ones).astype(jnp.int32)
        for i in range(per):
            g = q * per + i
            core, ch = g % 2, g // 2
            for s in range(steps):
                at = ((ch % pairs + 2 * pairs - 2 * core - pairs // 2 * s) % pairs) * unit
                idm[core, s, pl.ds(at + ch // pairs * rows, rows), :] = col[
                    i * rows : (i + 1) * rows, :
                ]
    lane = iota((nlow, 128), 1)
    lane1 = iota((1, 128), 1)
    tri = (iota((nlow, nlow), 1) < iota((nlow, nlow), 0)).astype(F32).astype(BF)
    jb = dp // 4
    for s in range(steps):
        for blk_id, core, ref in ((jb, c, psrc.at[s]), (t, c, pdst.at[0, s]), (t, 1 - c, pdst.at[1, s])):
            member = (idm[core, s] // 16) == blk_id
            rank = dot(tri, member.astype(F32).astype(BF)).astype(jnp.int32)
            ref[...] = jnp.where(member & (rank == lane), 1.0, 0.0).astype(BF)
    scl[c] = jnp.broadcast_to(
        jnp.where(
            lane1 < 64,
            jnp.where(lane1 < 32, scale_ref[0], scale_ref[1]),
            jnp.where(lane1 < 96, scale_ref[2], scale_ref[3]),
        ),
        (8, 128),
    )

    pl.semaphore_wait(barrier, nchip - 1 + 1 + nz - 1)

    def send(src, dst, ssem, rsem, dev):
        return pltpu.make_async_remote_copy(
            src_ref=src,
            dst_ref=dst,
            send_sem=ssem,
            recv_sem=rsem,
            device_id=dev,
            device_id_type=MESH,
        )

    waits = []

    def go(src, dst, ssem, rsem, dev):
        cp = send(src, dst, ssem, rsem, dev)
        cp.start()
        waits.append(cp)

    def got(ref, rsem):
        send(ref, ref, wsem.at[0], rsem, sibling).wait_recv()

    a = x * (1 - c) + y * c
    b = y * (1 - c) + x * c

    def chip_at(ca, cb):
        return (ca * c + cb * (1 - c)) * nx + ca * (1 - c) + cb * c

    def block(d, e, s):
        return rows_of(chip_at((a + nx - d) % nx, (b + nx - e) % nx), c, s, 0)

    others = (1, 3, 2)

    def share(d, src, s):
        blk = block(d, 0, s)
        for e in others:
            go(src, blk, ag2_s.at[s, d, e - 1], ag2_r.at[s, d, e - 1], peer(chip_at(a, (b + e) % nx)))

    def first_hop(s):
        for d in others:
            go(
                x_hbm.at[s],
                block(0, 0, s),
                ag1_s.at[s, d - 1],
                ag1_r.at[s, d - 1],
                peer(chip_at((a + d) % nx, b)),
            )
        share(0, x_hbm.at[s], s)

    def second_hop(s):
        for d in others:
            got(block(d, 0, s), ag1_r.at[s, d - 1])
            share(d, block(d, 0, s), s)

    def chunk(h, s):
        return xg.at[:, pl.ds((2 * h + s) * unit, unit), :]

    def swap(s):
        for d in (0, 1, 3, 2):
            for e in others:
                got(block(d, e, s), ag2_r.at[s, d, e - 1])
        mine[s].wait()
        go(chunk(0, s), chunk(1, s), sib_s.at[s], sib_r.at[s], sibling)

    def swapped(s):
        got(chunk(1, s), sib_r.at[s])

    nshard = xg.shape[0]
    root = t == jb
    rel_z = (t + nz - jb) % nz
    fr, fc = iota((128, 128), 0), iota((128, 128), 1)
    slots = 32

    def shrink(s):
        def one(i, _):
            n = 4
            rws = jnp.concatenate(
                [xg[n * i + z, s * unit : (s + 1) * unit, :] for z in range(n)], axis=0
            )
            at = pl.ds(pl.multiple_of(i * n * unit, n * unit), n * unit)
            total = jnp.zeros((n * unit, 128), F32)
            for core in range(2):
                keep = idm[c, s, at, :] == chip * 8 + core * 4 + lane1 // 32
                total = total + jnp.where(keep, dot(rws, ws[core]) * scl[core, 0:1, :], 0.0)
            masked[at, :] = total.astype(BF)
            return 0

        lax.fori_loop(0, nshard // 4, one, 0)
        comp = dot0(psrc[s], masked[...]).astype(BF)
        packed = jnp.zeros((slots, 128), F32)
        for q in range(4):
            fold = ((fr % 32 == fc % 32) & (fc // 32 == q)).astype(F32).astype(BF)
            packed = packed + dot(comp[slots * q : slots * (q + 1)], fold)
        lsend[s] = packed.astype(BF)

        @pl.when(jnp.logical_not(root))
        def _():
            send(
                lsend.at[s],
                lrecv.at[s, rel_z - 1],
                lz_s.at[s],
                lz_r.at[s, rel_z - 1],
                {"dp": dp, "tensor": jb},
            ).start()

    def root_sum(s):
        @pl.when(root)
        def _():
            total = lsend[s].astype(F32)
            for r in range(nz - 1):
                got(lrecv.at[s, r], lz_r.at[s, r])
                total = total + lrecv[s, r].astype(F32)
            lbc[s, x % 2] = total.astype(BF)
            for r in range(1, nchip):
                send(
                    lbc.at[s, x % 2],
                    lbc.at[s, x % 2],
                    lb_s.at[s, r - 1],
                    lb_r.at[s, x % 2],
                    peer((chip + r) % nchip),
                ).start()

    tr, tc = iota((128, 256), 0), iota((128, 256), 1)

    def take_low(s):
        for xi in range(2):

            @pl.when(chip != t * 2 + xi)
            def _():
                got(lbc.at[s, xi], lb_r.at[s, xi])

        low[0, s] = (lbc[s, 0].astype(F32) + lbc[s, 1].astype(F32)).astype(BF)
        go(low.at[0, s], low.at[1, s], lbs_s.at[s], lbs_r.at[s], sibling)

    def spread(h, s):
        if h == 1:
            got(low.at[1, s], lbs_r.at[s])
        core = c if h == 0 else 1 - c
        q = 2 * h + s
        for u in range(2):
            parts = []
            for z in range(4):
                pick = (tr == 32 * z + 16 * u + tc % 16).astype(F32).astype(BF)
                parts.append(dot(low[h, s], pick).astype(BF))
            tiled = jnp.concatenate(parts, axis=0)
            for w in range(2):
                wide = dot(pdst[h, s], tiled[:, w * 128 : w * 128 + 128])
                keep = idm[core, s] == t * 16 + w * 8 + lane // 16
                wide = jnp.where(keep, wide, 0.0).astype(BF)
                for p in range(nshard):
                    lowx[u, p, pl.ds(q * unit, unit), pl.ds(w * 128, 128)] = wide[
                        p * unit : (p + 1) * unit
                    ]

    def base(k):
        pg[k % 2] = dot(xg[(t + nz - 1 - k) % nz], wg[...])
        pu[k % 2] = dot(xg[(t + 1 + k) % nz], wu[...])

    def delta(k, at, size):
        part = pl.ds(at, size)
        pg[k % 2, part] += dot(lowx[0, (t + nz - 1 - k) % nz, at : at + size], we[0])
        pu[k % 2, part] += dot(lowx[1, (t + 1 + k) % nz, at : at + size], we[1])

    def ring_copy(k, u, q):
        buf = ru if u else rg
        part = pl.ds(q * unit, unit)
        return send(
            buf.at[k, part],
            buf.at[k + 1, part],
            rz_s.at[u, q, k],
            rz_r.at[u, q, k],
            plane(t + (nz - 1 if u else 1)),
        )

    def ring_start(q):
        delta(0, q * unit, unit)
        part = pl.ds(q * unit, unit)
        for u in range(2):
            buf, add = (ru, pu) if u else (rg, pg)
            buf[0, part] = add[0, part].astype(BF)
            ring_copy(0, u, q).start()

    def ring(k, h):
        delta(k, h * span, span)
        for q in (2 * h, 2 * h + 1):
            part = pl.ds(q * unit, unit)
            for u in range(2):
                buf, add = (ru, pu) if u else (rg, pg)
                ring_copy(k - 1, u, q).wait_recv()
                buf[k, part] = (buf[k, part].astype(F32) + add[k % 2, part]).astype(BF)
                ring_copy(k, u, q).start()

    def gather_copy(v, d, s):
        shard = (t + nz - d) % nz if v == 0 else (t + d) % nz
        ref = hid.at[shard, pl.ds(s * span, span)]
        return send(
            ref, ref, az_s.at[v, s, d], az_r.at[v, s, d], plane(t + (1 if v == 0 else nz - 1))
        )

    def finish(h):
        delta(nz - 1, h * span, span)
        part = pl.ds(h * span, span)
        for q in (2 * h, 2 * h + 1):
            for u in range(2):
                ring_copy(nz - 2, u, q).wait_recv()
        gate = rg[nz - 1, part].astype(F32) + pg[(nz - 1) % 2, part]
        up = ru[nz - 1, part].astype(F32) + pu[(nz - 1) % 2, part]
        hid[t, part] = (gate / (1.0 + jnp.exp(-gate)) * up).astype(BF)
        for v in range(2):
            cp = gather_copy(v, 0, h)
            cp.start()
            waits.append(cp)

    go(ws_hbm, ws.at[c], sw_s.at[0], sw_r.at[0], sibling)
    go(scl.at[c], scl.at[c], sw_s.at[1], sw_r.at[1], sibling)
    first_hop(0)
    first_hop(1)
    second_hop(0)
    second_hop(1)
    swap(0)
    loads[0].wait()
    got(ws.at[1 - c], sw_r.at[0])
    got(scl.at[1 - c], sw_r.at[1])
    shrink(0)
    swap(1)
    shrink(1)
    root_sum(0)
    for load in loads[1:4]:
        load.wait()
    swapped(0)
    swapped(1)
    base(0)
    root_sum(1)
    take_low(0)
    spread(0, 0)
    ring_start(0)
    take_low(1)
    spread(0, 1)
    ring_start(1)
    base(1)
    spread(1, 0)
    ring_start(2)
    ring(1, 0)
    spread(1, 1)
    ring_start(3)

    def slot_pair(k, _):
        base(k)
        ring(k, 0)
        ring(k - 1, 1)
        return 0

    lax.fori_loop(2, nz - 1, slot_pair, 0)
    base(nz - 1)
    finish(0)
    ring(nz - 2, 1)
    finish(1)
    loads[4].wait()

    far = nz // 2

    def down(shard, n):
        val = dot(hid[shard], wd[...]).astype(BF)
        for i in range(8):
            dbuf[n, i] = val[i * rows : (i + 1) * rows]
        go(dbuf.at[n, pl.ds(4, 4)], sbuf.at[n], sr_s.at[n], sr_r.at[n], sibling)

    def home_chip(shard, i):
        return (shard + 2 * c + pairs // 2 * (i // 2)) % pairs + pairs * (i % 2)

    def scatter_copy(shard, n, i):
        hc = home_chip(shard, i)
        rel = (chip + nchip - hc) % nchip
        return send(
            dbuf.at[n, i],
            rsb.at[i // 2, rel - 1],
            rs_s.at[n, i],
            rs_r.at[i // 2, rel - 1],
            peer(hc),
        )

    def scatter(shard, n):
        got(sbuf.at[n], sr_r.at[n])
        for i in range(4):
            total = dbuf[n, i].astype(F32) + sbuf[n, i].astype(F32)
            at_home = home_chip(shard, i) == chip

            @pl.when(at_home)
            def _():
                own[i // 2] = total

            @pl.when(jnp.logical_not(at_home))
            def _():
                dbuf[n, i] = total.astype(BF)
                scatter_copy(shard, n, i).start()

    down(t, 0)
    scatter(t, 0)
    pending = [(t, 0)]
    n = 1
    done = 1
    for d in range(1, far + 1):
        for s in range(steps):
            for v in range(2):
                if d == far and v != s:
                    continue
                shard = (t + nz - d) % nz if v == 0 else (t + d) % nz
                got(hid.at[shard, pl.ds(s * span, span)], az_r.at[v, s, d - 1])
                if d < far - 1 or (d == far - 1 and v == s):
                    cp = gather_copy(v, d, s)
                    cp.start()
                    waits.append(cp)
        todo = [(t + nz - d) % nz, (t + d) % nz] if d < far else [(t + far) % nz]
        for shard in todo:
            down(shard, n)
            pending.append((shard, n))
            n += 1
        for entry in pending[done:]:
            scatter(*entry)
        done = n

    for s in range(steps):
        total = own[s]
        for r in range(nchip - 1):
            got(rsb.at[s, r], rs_r.at[s, r])
            total = total + rsb[s, r].astype(F32)
        out_ref[s] = total.astype(BF)

    for cp in waits:
        cp.wait_send()
    for k in range(nz - 1):
        for q in range(2 * steps):
            for u in range(2):
                ring_copy(k, u, q).wait_send()
    for s in range(steps):

        @pl.when(jnp.logical_not(root))
        def _():
            send(lsend.at[s], lrecv.at[s, 0], lz_s.at[s], lz_r.at[s, 0], sibling).wait_send()

        @pl.when(root)
        def _():
            for r in range(1, nchip):
                send(
                    lbc.at[s, 0], lbc.at[s, 0], lb_s.at[s, r - 1], lb_r.at[s, 0], sibling
                ).wait_send()

    for shard, n in pending:
        for i in range(4):

            @pl.when(home_chip(shard, i) != chip)
            def _():
                scatter_copy(shard, n, i).wait_send()


def per_device(nx, ny, nz, act, wg, wu, wd, ws, we, scale, ids):
    steps, rows, feat = act.shape
    ff = wg.shape[1]
    dout = wd.shape[1]
    nrow = ids.shape[0]
    we = we.reshape(2, we.shape[1] * we.shape[2], ff)
    ids2 = ids.reshape(nrow // 128, 128)
    dma = pltpu.SemaphoreType.DMA
    nshard = 2 * nx
    chips = nx * ny
    nlow = chips * rows
    both = nrow * steps // nshard
    anyspec = pl.BlockSpec(memory_space=pl.ANY)
    vmem = pl.BlockSpec(memory_space=pltpu.VMEM)
    return pl.pallas_call(
        functools.partial(layer_kernel, nx, ny, nz),
        out_shape=jax.ShapeDtypeStruct((steps, rows, dout), BF),
        in_specs=[anyspec] * 6 + [pl.BlockSpec(memory_space=pltpu.SMEM), vmem],
        out_specs=vmem,
        scratch_shapes=[
            pltpu.VMEM((nshard, both, feat), BF),
            pltpu.VMEM(wg.shape, BF),
            pltpu.VMEM(wu.shape, BF),
            pltpu.VMEM(wd.shape, BF),
            pltpu.VMEM((2,) + ws.shape, BF),
            pltpu.VMEM((2, 8, 128), F32),
            pltpu.VMEM(we.shape, BF),
            pltpu.VMEM((2, steps, nlow, 128), jnp.int32),
            pltpu.VMEM((steps, nlow, 128), BF),
            pltpu.VMEM((2, steps, nlow, 128), BF),
            pltpu.VMEM((nlow, 128), BF),
            pltpu.VMEM((steps, 32, 128), BF),
            pltpu.VMEM((steps, nz - 1, 32, 128), BF),
            pltpu.VMEM((steps, 2, 32, 128), BF),
            pltpu.VMEM((2, steps, 32, 128), BF),
            pltpu.VMEM((2, nshard, both, 256), BF),
            pltpu.VMEM((2, both, ff), F32),
            pltpu.VMEM((2, both, ff), F32),
            pltpu.VMEM((nz, both, ff), BF),
            pltpu.VMEM((nz, both, ff), BF),
            pltpu.VMEM((nz, both, ff), BF),
            pltpu.VMEM((nshard, 8, rows, dout), BF),
            pltpu.VMEM((nshard, 4, rows, dout), BF),
            pltpu.VMEM((steps, chips - 1, rows, dout), BF),
            pltpu.VMEM((steps, rows, dout), F32),
            dma((5,)),
            dma((steps,)),
            dma((steps, 3)),
            dma((steps, 3)),
            dma((steps, 4, 3)),
            dma((steps, 4, 3)),
            dma((steps,)),
            dma((steps,)),
            dma((2,)),
            dma((2,)),
            dma((steps,)),
            dma((steps, nz - 1)),
            dma((steps, chips - 1)),
            dma((steps, 2)),
            dma((steps,)),
            dma((steps,)),
            dma((2, 2 * steps, nz - 1)),
            dma((2, 2 * steps, nz - 1)),
            dma((2, 2, 4)),
            dma((2, 2, 4)),
            dma((nshard,)),
            dma((nshard,)),
            dma((nshard, 4)),
            dma((steps, chips - 1)),
        ],
        compiler_params=pltpu.CompilerParams(
            collective_id=0, has_side_effects=True, vmem_limit_bytes=60 * 1024 * 1024
        ),
        name="layer",
    )(act, wg, wu, wd, ws, we, scale, ids2)


def solution(mesh):
    placed = (
        jax.sharding.PartitionSpec(None, "dp", "tensor"),
        jax.sharding.PartitionSpec("tensor", "dp"),
        jax.sharding.PartitionSpec("tensor", "dp"),
        jax.sharding.PartitionSpec("dp", "tensor"),
        jax.sharding.PartitionSpec("tensor", "dp"),
        jax.sharding.PartitionSpec(None, "tensor", None, "dp"),
        jax.sharding.PartitionSpec("dp"),
        jax.sharding.PartitionSpec(),
    )
    return jax.shard_map(
        functools.partial(per_device, 4, 4, mesh.shape["tensor"]),
        mesh=mesh,
        in_specs=placed,
        out_specs=jax.sharding.PartitionSpec(None, "dp", "tensor"),
        check_vma=False,
    )
```

```python
import functools

import jax
import jax.numpy as jnp
from jax import lax
from jax.experimental import pallas as pl
from jax.experimental.pallas import tpu as pltpu

MESH = pl.DeviceIdType.MESH
BF = jnp.bfloat16
F32 = jnp.float32


def dot(a, b):
    return jnp.dot(a, b, preferred_element_type=F32)


def dot0(a, b):
    return lax.dot_general(a, b, (((0,), (0,)), ((), ())), preferred_element_type=F32)


def iota(shape, dim):
    return lax.broadcasted_iota(jnp.int32, shape, dim)


def layer_kernel(
    nx,
    ny,
    nz,
    x_hbm,
    wg_hbm,
    wu_hbm,
    wd_hbm,
    ws_hbm,
    we_hbm,
    scale_ref,
    ids_ref,
    out_ref,
    xg,
    wg,
    wu,
    wd,
    ws,
    scl,
    we,
    idm,
    psrc,
    pdst,
    pnext,
    amask,
    pick,
    fold,
    lsend,
    lrecv,
    lbc,
    low,
    lowx,
    lowx1,
    wz,
    pg,
    pu,
    rg,
    ru,
    hid,
    dbuf,
    sbuf,
    rsb,
    own,
    wsem,
    lsem,
    ag1_s,
    ag1_r,
    ag2_s,
    ag2_r,
    sib_s,
    sib_r,
    sw_s,
    sw_r,
    lz_s,
    lz_r,
    lb_s,
    lb_r,
    lbs_s,
    lbs_r,
    ez_s,
    ez_r,
    rz_s,
    rz_r,
    az_s,
    az_r,
    sr_s,
    sr_r,
    rs_s,
    rs_r,
):
    nchip = nx * ny
    steps, rows, feat = x_hbm.shape
    pairs = nchip // 2
    unit = 2 * rows
    span = steps * unit
    dp = lax.axis_index("dp")
    t = lax.axis_index("tensor")
    c = dp % 2
    chip = dp // 2
    x = chip % nx
    y = chip // nx

    def shard_of(ch, core, s):
        return (ch % pairs + 2 * pairs - 2 * core - pairs // 2 * s) % pairs

    def rows_of(ch, core, s, h):
        at = (2 * h + s) * unit + ch // pairs * rows
        return xg.at[shard_of(ch, core, s), pl.ds(at, rows), :]

    mine = [
        pltpu.make_async_copy(x_hbm.at[s], rows_of(chip, c, s, 0), lsem.at[s])
        for s in range(steps)
    ]
    loads = [
        pltpu.make_async_copy(ws_hbm, ws.at[:, pl.ds(pl.multiple_of(c * 128, 128), 128)], wsem.at[0]),
        pltpu.make_async_copy(wg_hbm, wg, wsem.at[1]),
        pltpu.make_async_copy(wu_hbm, wu, wsem.at[2]),
        pltpu.make_async_copy(we_hbm, we, wsem.at[3]),
        pltpu.make_async_copy(wd_hbm, wd, wsem.at[4]),
    ]
    for load in mine + loads:
        load.start()

    def peer(chip_to):
        return {"dp": chip_to * 2 + c, "tensor": t}

    sibling = {"dp": chip * 2 + 1 - c, "tensor": t}

    def plane(z):
        return {"dp": dp, "tensor": z % nz}

    barrier = pltpu.get_barrier_semaphore()
    for rel in range(1, nchip):
        pl.semaphore_signal(
            barrier, inc=1, device_id=peer((chip + rel) % nchip), device_id_type=MESH
        )
    pl.semaphore_signal(barrier, inc=1, device_id=sibling, device_id_type=MESH)
    for rel in range(1, nz):
        pl.semaphore_signal(barrier, inc=1, device_id=plane(t + rel), device_id_type=MESH)

    eye = iota((128, 128), 0) == iota((128, 128), 1)
    ones = jnp.ones((128, 128), BF)
    per = 128 // rows
    nlow = idm.shape[2]
    for q in range(ids_ref.shape[0]):
        line = jnp.broadcast_to(ids_ref[pl.ds(q, 1), :], (128, 128))
        diag = jnp.where(eye, line, 0).astype(F32).astype(BF)
        col = dot(diag, ones).astype(jnp.int32)
        for i in range(per):
            g = q * per + i
            core, ch = g % 2, g // 2
            for s in range(steps):
                at = ((ch % pairs + 2 * pairs - 2 * core - pairs // 2 * s) % pairs) * unit
                idm[core, s, pl.ds(at + ch // pairs * rows, rows), :] = col[
                    i * rows : (i + 1) * rows, :
                ]
    lane = iota((nlow, 128), 1)
    lane1 = iota((1, 128), 1)
    tri = (iota((nlow, nlow), 1) < iota((nlow, nlow), 0)).astype(F32).astype(BF)
    jb = dp // 4

    def slot_table(core, s, blk_id):
        member = (idm[core, s] // 16) == blk_id
        rank = dot(tri, member.astype(F32).astype(BF)).astype(jnp.int32)
        return jnp.where(member & (rank == lane), 1.0, 0.0)

    def tables(h):
        core = c if h == 0 else 1 - c
        for s in range(steps):
            pdst[h, s] = slot_table(core, s, t).astype(BF)
            pnext[0, h, s] = slot_table(core, s, (t + nz - 1) % nz).astype(BF)
            pnext[1, h, s] = slot_table(core, s, (t + 1) % nz).astype(BF)
            for w in range(2):
                amask[h, s, :, pl.ds(w * 128, 128)] = (
                    (idm[core, s] % 16 == w * 8 + lane // 16).astype(F32).astype(BF)
                )

    for s in range(steps):
        psrc[s] = slot_table(c, s, jb).T.astype(BF)

    fr, fc = iota((128, 128), 0), iota((128, 128), 1)
    for u in range(2):
        fold[u] = (fr % 32 == 16 * u + fc % 16).astype(F32).astype(BF)
    tr, tc = iota((128, 256), 0), iota((128, 256), 1)
    pick[...] = (tr % 16 == tc % 16).astype(F32).astype(BF)
    group = fr // 16 == fc // 16
    scl[c] = jnp.broadcast_to(
        jnp.where(
            lane1 < 64,
            jnp.where(lane1 < 32, scale_ref[0], scale_ref[1]),
            jnp.where(lane1 < 96, scale_ref[2], scale_ref[3]),
        ),
        (8, 128),
    )

    pl.semaphore_wait(barrier, nchip - 1 + 1 + nz - 1)

    def send(src, dst, ssem, rsem, dev):
        return pltpu.make_async_remote_copy(
            src_ref=src,
            dst_ref=dst,
            send_sem=ssem,
            recv_sem=rsem,
            device_id=dev,
            device_id_type=MESH,
        )

    waits = []

    def go(src, dst, ssem, rsem, dev):
        cp = send(src, dst, ssem, rsem, dev)
        cp.start()
        waits.append(cp)

    def got(ref, rsem):
        send(ref, ref, wsem.at[0], rsem, sibling).wait_recv()

    a = x * (1 - c) + y * c
    b = y * (1 - c) + x * c

    def chip_at(ca, cb):
        return (ca * c + cb * (1 - c)) * nx + ca * (1 - c) + cb * c

    def block(d, e, s):
        return rows_of(chip_at((a + nx - d) % nx, (b + nx - e) % nx), c, s, 0)

    others = (1, 3, 2)

    def share(d, src, s):
        blk = block(d, 0, s)
        for e in others:
            go(src, blk, ag2_s.at[s, d, e - 1], ag2_r.at[s, d, e - 1], peer(chip_at(a, (b + e) % nx)))

    def first_hop(s):
        for d in others:
            go(
                x_hbm.at[s],
                block(0, 0, s),
                ag1_s.at[s, d - 1],
                ag1_r.at[s, d - 1],
                peer(chip_at((a + d) % nx, b)),
            )
        share(0, x_hbm.at[s], s)

    def second_hop(s):
        for d in others:
            got(block(d, 0, s), ag1_r.at[s, d - 1])
            share(d, block(d, 0, s), s)

    def chunk(h, s):
        return xg.at[:, pl.ds((2 * h + s) * unit, unit), :]

    def swap(s):
        for d in (0, 1, 3, 2):
            for e in others:
                blk = block(d, e, s)
                got(blk, ag2_r.at[s, d, e - 1])
        mine[s].wait()
        go(chunk(0, s), chunk(1, s), sib_s.at[s], sib_r.at[s], sibling)

    def swapped(s):
        got(chunk(1, s), sib_r.at[s])

    nshard = xg.shape[0]
    rel_z = (t + nz - jb) % nz
    kind = (rel_z + 1) % nz
    near = (0, 1, nz - 1)
    parts = {0: pl.ds(1, 1), 1: pl.ds(0, 2), 2: pl.ds(0, 1)}

    def shrink(s):
        rws = jnp.concatenate(
            [xg[z, s * unit : (s + 1) * unit, :] for z in range(nshard)], axis=0
        )
        shr = dot(rws, ws[...])
        total = jnp.zeros((nlow, 128), F32)
        for core in range(2):
            keep = idm[c, s] == chip * 8 + core * 4 + lane1 // 32
            total = total + jnp.where(
                keep, shr[:, core * 128 : core * 128 + 128] * scl[core, 0:1, :], 0.0
            )
        comp = dot(psrc[s], total.astype(BF)).astype(BF)
        for u in range(2):
            wide = jnp.where(group, dot(comp, fold[u]), 0.0)
            packed = wide[:16]
            for q in range(1, 8):
                packed = packed + wide[16 * q : 16 * (q + 1)]
            lsend[s, u] = packed.astype(BF)

        for o in range(3):

            @pl.when(rel_z != near[o])
            def _():
                low_copy(s, o).start()

    def low_copy(s, o):
        slot = (rel_z + nz - near[o]) % nz - 1
        us = parts[(1, 2, 0)[o]]
        return send(
            lsend.at[s, us],
            lrecv.at[s, slot, us],
            lz_s.at[s, o],
            lz_r.at[s, slot],
            plane(jb + near[o]),
        )

    def low_out(s, i, r):
        ref = lbc.at[s, i, x % 2, parts[i]]
        return send(
            ref, ref, lb_s.at[s, r - 1], lb_r.at[s, i, x % 2], peer((chip + r) % nchip)
        )

    def root_sum(s):
        for i in range(3):

            @pl.when(kind == i)
            def _():
                us = parts[i]
                total = lsend[s, us].astype(F32)
                for r in range(nz - 1):
                    got(lrecv.at[s, r, us], lz_r.at[s, r])
                    total = total + lrecv[s, r, us].astype(F32)
                lbc[s, i, x % 2, us] = total.astype(BF)
                for r in range(1, nchip):
                    low_out(s, i, r).start()

    def take_low(s, i):
        blk_id = (t + 1 + nz - i) % nz
        for xi in range(2):

            @pl.when(chip != blk_id * 2 + xi)
            def _():
                got(lbc.at[s, i, xi, parts[i]], lb_r.at[s, i, xi])

        us = parts[i]
        low[0, s, i, us] = (lbc[s, i, 0, us].astype(F32) + lbc[s, i, 1, us].astype(F32)).astype(BF)
        go(low.at[0, s, i, us], low.at[1, s, i, us], lbs_s.at[s, i], lbs_r.at[s, i], sibling)

    def late_low():
        for i in range(3):
            for s in range(steps):
                got(low.at[1, s, i, parts[i]], lbs_r.at[s, i])

    def widen(vec):
        rows8 = jnp.concatenate([vec] * 8, axis=0)
        return dot(jnp.where(group, rows8, jnp.zeros_like(rows8)), pick[...]).astype(BF)

    def spread_next(h):
        for u in range(2):
            shard = (t + 2 * nz - 2) % nz if u == 0 else (t + 2) % nz
            at = pl.ds(pl.multiple_of(shard * unit, unit), unit)
            for s in range(steps):
                tiled = widen(low[h, s, 2 - 2 * u, u])
                wide = dot(pnext[u, h, s, at, :], tiled)
                lowx1[u, pl.ds((2 * h + s) * unit, unit)] = wide.astype(BF) * amask[h, s, at, :]
        part = pl.ds(h * span, span)
        pg[1, part] += dot(lowx1[0, part], wz[0])
        pu[1, part] += dot(lowx1[1, part], wz[1])

    def spread(h, s):
        q = 2 * h + s
        for u in range(2):
            part = dot(pdst[h, s], widen(low[h, s, 1, u])).astype(BF) * amask[h, s]
            for p in range(nshard):
                lowx[u, p, pl.ds(q * unit, unit)] = part[p * unit : (p + 1) * unit]

    def base(k):
        pg[k % 2] = dot(xg[(t + nz - 1 - k) % nz], wg[...])
        pu[k % 2] = dot(xg[(t + 1 + k) % nz], wu[...])

    def base_first(h):
        part = pl.ds(h * span, span)
        pg[0, part] = dot(xg[(t + nz - 1) % nz, part], wg[...])
        pu[0, part] = dot(xg[(t + 1) % nz, part], wu[...])

    def delta(k, at, size):
        part = pl.ds(at, size)
        pg[k % 2, part] += dot(lowx[0, (t + nz - 1 - k) % nz, at : at + size], we[0])
        pu[k % 2, part] += dot(lowx[1, (t + 1 + k) % nz, at : at + size], we[1])

    def ring_copy(k, u, q):
        buf = ru if u else rg
        part = pl.ds(q * unit, unit)
        return send(
            buf.at[k, part],
            buf.at[k + 1, part],
            rz_s.at[u, q, k],
            rz_r.at[u, q, k],
            plane(t + (nz - 1 if u else 1)),
        )

    def ring_start(q):
        part = pl.ds(q * unit, unit)
        for u in range(2):
            buf, add = (ru, pu) if u else (rg, pg)
            buf[0, part] = add[0, part].astype(BF)
            ring_copy(0, u, q).start()

    def ring(k, h):
        delta(k, h * span, span)
        for q in (2 * h, 2 * h + 1):
            part = pl.ds(q * unit, unit)
            for u in range(2):
                buf, add = (ru, pu) if u else (rg, pg)
                ring_copy(k - 1, u, q).wait_recv()
                buf[k, part] = (buf[k, part].astype(F32) + add[k % 2, part]).astype(BF)
                ring_copy(k, u, q).start()

    def gather_copy(v, d, s):
        shard = (t + nz - d) % nz if v == 0 else (t + d) % nz
        ref = hid.at[shard, pl.ds(s * span, span)]
        return send(
            ref, ref, az_s.at[v, s, d], az_r.at[v, s, d], plane(t + (1 if v == 0 else nz - 1))
        )

    def finish(h):
        delta(nz - 1, h * span, span)
        part = pl.ds(h * span, span)
        for q in (2 * h, 2 * h + 1):
            for u in range(2):
                ring_copy(nz - 2, u, q).wait_recv()
        gate = rg[nz - 1, part].astype(F32) + pg[(nz - 1) % 2, part]
        up = ru[nz - 1, part].astype(F32) + pu[(nz - 1) % 2, part]
        hid[t, part] = (gate / (1.0 + jnp.exp(-gate)) * up).astype(BF)
        for v in range(2):
            cp = gather_copy(v, 0, h)
            cp.start()
            waits.append(cp)

    ws_mine = ws.at[:, pl.ds(pl.multiple_of(c * 128, 128), 128)]
    ws_other = ws.at[:, pl.ds(pl.multiple_of(128 - c * 128, 128), 128)]
    go(ws_hbm, ws_mine, sw_s.at[0], sw_r.at[0], sibling)
    go(scl.at[c], scl.at[c], sw_s.at[1], sw_r.at[1], sibling)
    first_hop(0)
    first_hop(1)
    for u in range(2):
        dev = plane(t + (nz - 1 if u else 1))
        go(we_hbm.at[u], wz.at[u], ez_s.at[u], ez_r.at[u], dev)
    tables(0)
    second_hop(0)
    second_hop(1)
    tables(1)
    swap(0)
    loads[0].wait()
    got(ws_other, sw_r.at[0])
    got(scl.at[1 - c], sw_r.at[1])
    shrink(0)
    swap(1)
    shrink(1)
    for load in loads[1:4]:
        load.wait()
    root_sum(0)
    base_first(0)
    ring_start(0)
    ring_start(1)
    root_sum(1)
    swapped(0)
    swapped(1)
    base_first(1)
    ring_start(2)
    ring_start(3)
    base(1)
    for i in (1, 2, 0):
        for s in range(steps):
            take_low(s, i)
    for u in range(2):
        got(wz.at[u], ez_r.at[u])
    for s in range(steps):
        spread(0, s)
    spread_next(0)
    ring(1, 0)
    late_low()
    for s in range(steps):
        spread(1, s)
    spread_next(1)

    def slot_pair(k, _):
        base(k)
        ring(k, 0)
        ring(k - 1, 1)
        return 0

    lax.fori_loop(2, nz - 1, slot_pair, 0)
    base(nz - 1)
    finish(0)
    ring(nz - 2, 1)
    finish(1)
    loads[4].wait()

    far = nz // 2

    def down(shard, n):
        val = dot(hid[shard], wd[...]).astype(BF)
        for i in range(8):
            dbuf[n, i] = val[i * rows : (i + 1) * rows]
        go(dbuf.at[n, pl.ds(4, 4)], sbuf.at[n], sr_s.at[n], sr_r.at[n], sibling)

    def home_chip(shard, i):
        return (shard + 2 * c + pairs // 2 * (i // 2)) % pairs + pairs * (i % 2)

    def scatter_copy(shard, n, i):
        hc = home_chip(shard, i)
        rel = (chip + nchip - hc) % nchip
        return send(
            dbuf.at[n, i],
            rsb.at[i // 2, rel - 1],
            rs_s.at[n, i],
            rs_r.at[i // 2, rel - 1],
            peer(hc),
        )

    def scatter(shard, n):
        got(sbuf.at[n], sr_r.at[n])
        for i in range(4):
            total = dbuf[n, i].astype(F32) + sbuf[n, i].astype(F32)
            at_home = home_chip(shard, i) == chip

            @pl.when(at_home)
            def _():
                own[i // 2] = total

            @pl.when(jnp.logical_not(at_home))
            def _():
                dbuf[n, i] = total.astype(BF)
                scatter_copy(shard, n, i).start()

    down(t, 0)
    scatter(t, 0)
    pending = [(t, 0)]
    n = 1
    done = 1
    for d in range(1, far + 1):
        for s in range(steps):
            for v in range(2):
                if d == far and v != s:
                    continue
                shard = (t + nz - d) % nz if v == 0 else (t + d) % nz
                got(hid.at[shard, pl.ds(s * span, span)], az_r.at[v, s, d - 1])
                if d < far - 1 or (d == far - 1 and v == s):
                    cp = gather_copy(v, d, s)
                    cp.start()
                    waits.append(cp)
        todo = [(t + nz - d) % nz, (t + d) % nz] if d < far else [(t + far) % nz]
        for shard in todo:
            down(shard, n)
            pending.append((shard, n))
            n += 1
        for entry in pending[done:]:
            scatter(*entry)
        done = n

    for s in range(steps):
        total = own[s]
        for r in range(nchip - 1):
            got(rsb.at[s, r], rs_r.at[s, r])
            total = total + rsb[s, r].astype(F32)
        out_ref[s] = total.astype(BF)

    for cp in waits:
        cp.wait_send()
    for k in range(nz - 1):
        for q in range(2 * steps):
            for u in range(2):
                ring_copy(k, u, q).wait_send()
    for s in range(steps):

        for o in range(3):

            @pl.when(rel_z != near[o])
            def _():
                low_copy(s, o).wait_send()

        for i in range(3):

            @pl.when(kind == i)
            def _():
                for r in range(1, nchip):
                    low_out(s, i, r).wait_send()

    for shard, n in pending:
        for i in range(4):

            @pl.when(home_chip(shard, i) != chip)
            def _():
                scatter_copy(shard, n, i).wait_send()


def per_device(nx, ny, nz, act, wg, wu, wd, ws, we, scale, ids):
    steps, rows, feat = act.shape
    ff = wg.shape[1]
    dout = wd.shape[1]
    nrow = ids.shape[0]
    we = we.reshape(2, we.shape[1] * we.shape[2], ff)
    ids2 = ids.reshape(nrow // 128, 128)
    dma = pltpu.SemaphoreType.DMA
    nshard = 2 * nx
    chips = nx * ny
    nlow = chips * rows
    both = nrow * steps // nshard
    anyspec = pl.BlockSpec(memory_space=pl.ANY)
    vmem = pl.BlockSpec(memory_space=pltpu.VMEM)
    return pl.pallas_call(
        functools.partial(layer_kernel, nx, ny, nz),
        out_shape=jax.ShapeDtypeStruct((steps, rows, dout), BF),
        in_specs=[anyspec] * 6 + [pl.BlockSpec(memory_space=pltpu.SMEM), vmem],
        out_specs=vmem,
        scratch_shapes=[
            pltpu.VMEM((nshard, both, feat), BF),
            pltpu.VMEM(wg.shape, BF),
            pltpu.VMEM(wu.shape, BF),
            pltpu.VMEM(wd.shape, BF),
            pltpu.VMEM((ws.shape[0], 2 * ws.shape[1]), BF),
            pltpu.VMEM((2, 8, 128), F32),
            pltpu.VMEM(we.shape, BF),
            pltpu.VMEM((2, steps, nlow, 128), jnp.int32),
            pltpu.VMEM((steps, 128, nlow), BF),
            pltpu.VMEM((2, steps, nlow, 128), BF),
            pltpu.VMEM((2, 2, steps, nlow, 128), BF),
            pltpu.VMEM((2, steps, nlow, 256), BF),
            pltpu.VMEM((128, 256), BF),
            pltpu.VMEM((2, 128, 128), BF),
            pltpu.VMEM((steps, 2, 16, 128), BF),
            pltpu.VMEM((steps, nz - 1, 2, 16, 128), BF),
            pltpu.VMEM((steps, 3, 2, 2, 16, 128), BF),
            pltpu.VMEM((2, steps, 3, 2, 16, 128), BF),
            pltpu.VMEM((2, nshard, both, 256), BF),
            pltpu.VMEM((2, both, 256), BF),
            pltpu.VMEM(we.shape, BF),
            pltpu.VMEM((2, both, ff), F32),
            pltpu.VMEM((2, both, ff), F32),
            pltpu.VMEM((nz, both, ff), BF),
            pltpu.VMEM((nz, both, ff), BF),
            pltpu.VMEM((nz, both, ff), BF),
            pltpu.VMEM((nshard, 8, rows, dout), BF),
            pltpu.VMEM((nshard, 4, rows, dout), BF),
            pltpu.VMEM((steps, chips - 1, rows, dout), BF),
            pltpu.VMEM((steps, rows, dout), F32),
            dma((5,)),
            dma((steps,)),
            dma((steps, 3)),
            dma((steps, 3)),
            dma((steps, 4, 3)),
            dma((steps, 4, 3)),
            dma((steps,)),
            dma((steps,)),
            dma((2,)),
            dma((2,)),
            dma((steps, 3)),
            dma((steps, nz - 1)),
            dma((steps, chips - 1)),
            dma((steps, 3, 2)),
            dma((steps, 3)),
            dma((steps, 3)),
            dma((2,)),
            dma((2,)),
            dma((2, 2 * steps, nz - 1)),
            dma((2, 2 * steps, nz - 1)),
            dma((2, 2, 4)),
            dma((2, 2, 4)),
            dma((nshard,)),
            dma((nshard,)),
            dma((nshard, 4)),
            dma((steps, chips - 1)),
        ],
        compiler_params=pltpu.CompilerParams(
            collective_id=0, has_side_effects=True, vmem_limit_bytes=60 * 1024 * 1024
        ),
        name="layer",
    )(act, wg, wu, wd, ws, we, scale, ids2)


def solution(mesh):
    placed = (
        jax.sharding.PartitionSpec(None, "dp", "tensor"),
        jax.sharding.PartitionSpec("tensor", "dp"),
        jax.sharding.PartitionSpec("tensor", "dp"),
        jax.sharding.PartitionSpec("dp", "tensor"),
        jax.sharding.PartitionSpec("tensor", "dp"),
        jax.sharding.PartitionSpec(None, "tensor", None, "dp"),
        jax.sharding.PartitionSpec("dp"),
        jax.sharding.PartitionSpec(),
    )
    return jax.shard_map(
        functools.partial(per_device, 4, 4, mesh.shape["tensor"]),
        mesh=mesh,
        in_specs=placed,
        out_specs=jax.sharding.PartitionSpec(None, "dp", "tensor"),
        check_vma=False,
    )
```

```python
import functools

import jax
import jax.numpy as jnp
from jax import lax
from jax.experimental import pallas as pl
from jax.experimental.pallas import tpu as pltpu

MESH = pl.DeviceIdType.MESH
BF = jnp.bfloat16
F32 = jnp.float32
AHEAD = 3


def dot(a, b):
    return jnp.dot(a, b, preferred_element_type=F32)


def dot0(a, b):
    return lax.dot_general(a, b, (((0,), (0,)), ((), ())), preferred_element_type=F32)


def iota(shape, dim):
    return lax.broadcasted_iota(jnp.int32, shape, dim)


def layer_kernel(
    nx,
    ny,
    nz,
    x_hbm,
    wg_hbm,
    wu_hbm,
    wd_hbm,
    ws_hbm,
    we_hbm,
    scale_ref,
    ids_ref,
    out_ref,
    xg,
    wg,
    wu,
    wd,
    ws,
    scl,
    we,
    idm,
    psrc,
    pdst,
    pnext,
    amask,
    pick,
    fold,
    lsend,
    lrecv,
    lbc,
    low,
    lowx,
    lowx1,
    wz,
    pg,
    pu,
    rg,
    ru,
    hid,
    dbuf,
    sbuf,
    rsb,
    own,
    wsem,
    lsem,
    ag1_s,
    ag1_r,
    ag2_s,
    ag2_r,
    sib_s,
    sib_r,
    sw_s,
    sw_r,
    lz_s,
    lz_r,
    lb_s,
    lb_r,
    lbs_s,
    lbs_r,
    ez_s,
    ez_r,
    rz_s,
    rz_r,
    az_s,
    az_r,
    sr_s,
    sr_r,
    rs_s,
    rs_r,
):
    nchip = nx * ny
    steps, rows, feat = x_hbm.shape
    pairs = nchip // 2
    unit = 2 * rows
    span = steps * unit
    dp = lax.axis_index("dp")
    t = lax.axis_index("tensor")
    c = dp % 2
    chip = dp // 2
    x = chip % nx
    y = chip // nx

    def shard_of(ch, core, s):
        return (ch % pairs + 2 * pairs - 2 * core - pairs // 2 * s) % pairs

    def rows_of(ch, core, s, h):
        at = (2 * h + s) * unit + ch // pairs * rows
        return xg.at[shard_of(ch, core, s), pl.ds(at, rows), :]

    mine = [
        pltpu.make_async_copy(x_hbm.at[s], rows_of(chip, c, s, 0), lsem.at[s])
        for s in range(steps)
    ]
    loads = [
        pltpu.make_async_copy(ws_hbm, ws.at[:, pl.ds(pl.multiple_of(c * 128, 128), 128)], wsem.at[0]),
        pltpu.make_async_copy(wg_hbm, wg, wsem.at[1]),
        pltpu.make_async_copy(wu_hbm, wu, wsem.at[2]),
        pltpu.make_async_copy(we_hbm, we, wsem.at[3]),
        pltpu.make_async_copy(wd_hbm, wd, wsem.at[4]),
    ]
    for load in mine + loads:
        load.start()

    def peer(chip_to):
        return {"dp": chip_to * 2 + c, "tensor": t}

    sibling = {"dp": chip * 2 + 1 - c, "tensor": t}

    def plane(z):
        return {"dp": dp, "tensor": z % nz}

    barrier = pltpu.get_barrier_semaphore()
    for rel in range(1, nchip):
        pl.semaphore_signal(
            barrier, inc=1, device_id=peer((chip + rel) % nchip), device_id_type=MESH
        )
    pl.semaphore_signal(barrier, inc=1, device_id=sibling, device_id_type=MESH)
    for rel in range(1, nz):
        pl.semaphore_signal(barrier, inc=1, device_id=plane(t + rel), device_id_type=MESH)

    eye = iota((128, 128), 0) == iota((128, 128), 1)
    ones = jnp.ones((128, 128), BF)
    per = 128 // rows
    nlow = idm.shape[2]
    for q in range(ids_ref.shape[0]):
        line = jnp.broadcast_to(ids_ref[pl.ds(q, 1), :], (128, 128))
        diag = jnp.where(eye, line, 0).astype(F32).astype(BF)
        col = dot(diag, ones).astype(jnp.int32)
        for i in range(per):
            g = q * per + i
            core, ch = g % 2, g // 2
            for s in range(steps):
                at = ((ch % pairs + 2 * pairs - 2 * core - pairs // 2 * s) % pairs) * unit
                idm[core, s, pl.ds(at + ch // pairs * rows, rows), :] = col[
                    i * rows : (i + 1) * rows, :
                ]
    lane = iota((nlow, 128), 1)
    lane1 = iota((1, 128), 1)
    tri = (iota((nlow, nlow), 1) < iota((nlow, nlow), 0)).astype(F32).astype(BF)
    jb = dp // 4

    def slot_table(core, s, blk_id):
        member = (idm[core, s] // 16) == blk_id
        rank = dot(tri, member.astype(F32).astype(BF)).astype(jnp.int32)
        return jnp.where(member & (rank == lane), 1.0, 0.0)

    def tables(h):
        core = c if h == 0 else 1 - c
        for s in range(steps):
            pdst[h, s] = slot_table(core, s, t).astype(BF)
            pnext[0, h, s] = slot_table(core, s, (t + nz - 1) % nz).astype(BF)
            pnext[1, h, s] = slot_table(core, s, (t + 1) % nz).astype(BF)
            for w in range(2):
                amask[h, s, :, pl.ds(w * 128, 128)] = (
                    (idm[core, s] % 16 == w * 8 + lane // 16).astype(F32).astype(BF)
                )

    for s in range(steps):
        psrc[s] = slot_table(c, s, jb).T.astype(BF)

    fr, fc = iota((128, 128), 0), iota((128, 128), 1)
    for u in range(2):
        fold[u] = (fr % 32 == 16 * u + fc % 16).astype(F32).astype(BF)
    tr, tc = iota((128, 256), 0), iota((128, 256), 1)
    pick[...] = (tr % 16 == tc % 16).astype(F32).astype(BF)
    group = fr // 16 == fc // 16
    scl[c] = jnp.broadcast_to(
        jnp.where(
            lane1 < 64,
            jnp.where(lane1 < 32, scale_ref[0], scale_ref[1]),
            jnp.where(lane1 < 96, scale_ref[2], scale_ref[3]),
        ),
        (8, 128),
    )

    pl.semaphore_wait(barrier, nchip - 1 + 1 + nz - 1)

    def send(src, dst, ssem, rsem, dev):
        return pltpu.make_async_remote_copy(
            src_ref=src,
            dst_ref=dst,
            send_sem=ssem,
            recv_sem=rsem,
            device_id=dev,
            device_id_type=MESH,
        )

    waits = []

    def go(src, dst, ssem, rsem, dev):
        cp = send(src, dst, ssem, rsem, dev)
        cp.start()
        waits.append(cp)

    def got(ref, rsem):
        send(ref, ref, wsem.at[0], rsem, sibling).wait_recv()

    a = x * (1 - c) + y * c
    b = y * (1 - c) + x * c

    def chip_at(ca, cb):
        return (ca * c + cb * (1 - c)) * nx + ca * (1 - c) + cb * c

    def block(d, e, s):
        return rows_of(chip_at((a + nx - d) % nx, (b + nx - e) % nx), c, s, 0)

    others = (1, 3, 2)

    def share(d, src, s):
        blk = block(d, 0, s)
        for e in others:
            go(src, blk, ag2_s.at[s, d, e - 1], ag2_r.at[s, d, e - 1], peer(chip_at(a, (b + e) % nx)))

    def first_hop(s):
        for d in others:
            go(
                x_hbm.at[s],
                block(0, 0, s),
                ag1_s.at[s, d - 1],
                ag1_r.at[s, d - 1],
                peer(chip_at((a + d) % nx, b)),
            )
        share(0, x_hbm.at[s], s)

    def second_hop(s):
        for d in others:
            got(block(d, 0, s), ag1_r.at[s, d - 1])
            share(d, block(d, 0, s), s)

    def chunk(h, s):
        return xg.at[:, pl.ds((2 * h + s) * unit, unit), :]

    def swap(s):
        for d in (0, 1, 3, 2):
            for e in others:
                blk = block(d, e, s)
                got(blk, ag2_r.at[s, d, e - 1])
        mine[s].wait()
        go(chunk(0, s), chunk(1, s), sib_s.at[s], sib_r.at[s], sibling)

    def swapped(s):
        got(chunk(1, s), sib_r.at[s])

    nshard = xg.shape[0]
    rel_z = (t + nz - jb) % nz
    kind = (rel_z + 1) % nz
    near = (0, 1, nz - 1)
    parts = {0: pl.ds(1, 1), 1: pl.ds(0, 2), 2: pl.ds(0, 1)}

    def shrink(s):
        rws = jnp.concatenate(
            [xg[z, s * unit : (s + 1) * unit, :] for z in range(nshard)], axis=0
        )
        shr = dot(rws, ws[...])
        total = jnp.zeros((nlow, 128), F32)
        for core in range(2):
            keep = idm[c, s] == chip * 8 + core * 4 + lane1 // 32
            total = total + jnp.where(
                keep, shr[:, core * 128 : core * 128 + 128] * scl[core, 0:1, :], 0.0
            )
        comp = dot(psrc[s], total.astype(BF)).astype(BF)
        for u in range(2):
            wide = jnp.where(group, dot(comp, fold[u]), 0.0)
            packed = wide[:16]
            for q in range(1, 8):
                packed = packed + wide[16 * q : 16 * (q + 1)]
            lsend[s, u] = packed.astype(BF)

        for o in range(3):

            @pl.when(rel_z != near[o])
            def _():
                low_copy(s, o).start()

    def low_copy(s, o):
        slot = (rel_z + nz - near[o]) % nz - 1
        us = parts[(1, 2, 0)[o]]
        return send(
            lsend.at[s, us],
            lrecv.at[s, slot, us],
            lz_s.at[s, o],
            lz_r.at[s, slot],
            plane(jb + near[o]),
        )

    def low_out(s, i, r):
        ref = lbc.at[s, i, x % 2, parts[i]]
        return send(
            ref, ref, lb_s.at[s, r - 1], lb_r.at[s, i, x % 2], peer((chip + r) % nchip)
        )

    def root_sum(s):
        for i in range(3):

            @pl.when(kind == i)
            def _():
                us = parts[i]
                total = lsend[s, us].astype(F32)
                for r in range(nz - 1):
                    got(lrecv.at[s, r, us], lz_r.at[s, r])
                    total = total + lrecv[s, r, us].astype(F32)
                lbc[s, i, x % 2, us] = total.astype(BF)
                for r in range(1, nchip):
                    low_out(s, i, r).start()

    def take_low(s, i):
        blk_id = (t + 1 + nz - i) % nz
        for xi in range(2):

            @pl.when(chip != blk_id * 2 + xi)
            def _():
                got(lbc.at[s, i, xi, parts[i]], lb_r.at[s, i, xi])

        us = parts[i]
        low[0, s, i, us] = (lbc[s, i, 0, us].astype(F32) + lbc[s, i, 1, us].astype(F32)).astype(BF)
        go(low.at[0, s, i, us], low.at[1, s, i, us], lbs_s.at[s, i], lbs_r.at[s, i], sibling)

    def late_low():
        for i in range(3):
            for s in range(steps):
                got(low.at[1, s, i, parts[i]], lbs_r.at[s, i])

    def widen(vec):
        rows8 = jnp.concatenate([vec] * 8, axis=0)
        return dot(jnp.where(group, rows8, jnp.zeros_like(rows8)), pick[...]).astype(BF)

    def spread_next(h):
        for u in range(2):
            shard = (t + 2 * nz - 2) % nz if u == 0 else (t + 2) % nz
            at = pl.ds(pl.multiple_of(shard * unit, unit), unit)
            for s in range(steps):
                tiled = widen(low[h, s, 2 - 2 * u, u])
                wide = dot(pnext[u, h, s, at, :], tiled)
                lowx1[u, pl.ds((2 * h + s) * unit, unit)] = wide.astype(BF) * amask[h, s, at, :]
        part = pl.ds(h * span, span)
        pg[1, part] += dot(lowx1[0, part], wz[0])
        pu[1, part] += dot(lowx1[1, part], wz[1])

    def spread(h, s):
        q = 2 * h + s
        for u in range(2):
            part = dot(pdst[h, s], widen(low[h, s, 1, u])).astype(BF) * amask[h, s]
            for p in range(nshard):
                lowx[u, p, pl.ds(q * unit, unit)] = part[p * unit : (p + 1) * unit]

    def base(k):
        pg[k] = dot(xg[(t + nz - 1 - k) % nz], wg[...])
        pu[k] = dot(xg[(t + 1 + k) % nz], wu[...])

    def base_first(h):
        part = pl.ds(h * span, span)
        pg[0, part] = dot(xg[(t + nz - 1) % nz, part], wg[...])
        pu[0, part] = dot(xg[(t + 1) % nz, part], wu[...])

    def delta(k, at, size):
        part = pl.ds(at, size)
        pg[k, part] += dot(lowx[0, (t + nz - 1 - k) % nz, at : at + size], we[0])
        pu[k, part] += dot(lowx[1, (t + 1 + k) % nz, at : at + size], we[1])

    def ring_copy(k, u, q):
        buf = ru if u else rg
        part = pl.ds(q * unit, unit)
        return send(
            buf.at[k, part],
            buf.at[k + 1, part],
            rz_s.at[u, q, k],
            rz_r.at[u, q, k],
            plane(t + (nz - 1 if u else 1)),
        )

    def ring_start(q):
        part = pl.ds(q * unit, unit)
        for u in range(2):
            buf, add = (ru, pu) if u else (rg, pg)
            buf[0, part] = add[0, part].astype(BF)
            ring_copy(0, u, q).start()

    def ring(k, h):
        delta(k, h * span, span)
        for q in (2 * h, 2 * h + 1):
            part = pl.ds(q * unit, unit)
            for u in range(2):
                buf, add = (ru, pu) if u else (rg, pg)
                ring_copy(k - 1, u, q).wait_recv()
                buf[k, part] = (buf[k, part].astype(F32) + add[k, part]).astype(BF)
                ring_copy(k, u, q).start()

    def gather_copy(v, d, q):
        shard = (t + nz - d) % nz if v == 0 else (t + d) % nz
        ref = hid.at[shard, pl.ds(q * unit, unit)]
        return send(
            ref, ref, az_s.at[v, q, d], az_r.at[v, q, d], plane(t + (1 if v == 0 else nz - 1))
        )

    def finish(h):
        delta(nz - 1, h * span, span)
        for q in (2 * h, 2 * h + 1):
            part = pl.ds(q * unit, unit)
            for u in range(2):
                ring_copy(nz - 2, u, q).wait_recv()
            gate = rg[nz - 1, part].astype(F32) + pg[nz - 1, part]
            up = ru[nz - 1, part].astype(F32) + pu[nz - 1, part]
            hid[t, part] = (gate / (1.0 + jnp.exp(-gate)) * up).astype(BF)
            for v in range(2):
                cp = gather_copy(v, 0, q)
                cp.start()
                waits.append(cp)

    ws_mine = ws.at[:, pl.ds(pl.multiple_of(c * 128, 128), 128)]
    ws_other = ws.at[:, pl.ds(pl.multiple_of(128 - c * 128, 128), 128)]
    go(ws_hbm, ws_mine, sw_s.at[0], sw_r.at[0], sibling)
    go(scl.at[c], scl.at[c], sw_s.at[1], sw_r.at[1], sibling)
    first_hop(0)
    first_hop(1)
    for u in range(2):
        dev = plane(t + (nz - 1 if u else 1))
        go(we_hbm.at[u], wz.at[u], ez_s.at[u], ez_r.at[u], dev)
    tables(0)
    second_hop(0)
    second_hop(1)
    tables(1)
    swap(0)
    loads[0].wait()
    got(ws_other, sw_r.at[0])
    got(scl.at[1 - c], sw_r.at[1])
    shrink(0)
    swap(1)
    shrink(1)
    for load in loads[1:4]:
        load.wait()
    root_sum(0)
    base_first(0)
    ring_start(0)
    ring_start(1)
    root_sum(1)
    swapped(0)
    swapped(1)
    base_first(1)
    ring_start(2)
    ring_start(3)
    lax.fori_loop(1, AHEAD + 2, lambda k, _: base(k) or 0, 0)
    for i in (1, 2, 0):
        for s in range(steps):
            take_low(s, i)
    for u in range(2):
        got(wz.at[u], ez_r.at[u])
    for s in range(steps):
        spread(0, s)
    spread_next(0)
    ring(1, 0)
    late_low()
    for s in range(steps):
        spread(1, s)
    spread_next(1)

    def slot_pair(k, _):
        ring(k, 0)
        ring(k - 1, 1)

        @pl.when(k + AHEAD < nz)
        def _():
            base(k + AHEAD)

        return 0

    lax.fori_loop(2, nz - 1, slot_pair, 0)
    finish(0)
    ring(nz - 2, 1)
    finish(1)
    loads[4].wait()

    far = nz // 2

    def down(shard, n):
        val = dot(hid[shard], wd[...]).astype(BF)
        for i in range(8):
            dbuf[n, i] = val[i * rows : (i + 1) * rows]
        go(dbuf.at[n, pl.ds(4, 4)], sbuf.at[n], sr_s.at[n], sr_r.at[n], sibling)

    def home_chip(shard, i):
        return (shard + 2 * c + pairs // 2 * (i // 2)) % pairs + pairs * (i % 2)

    def scatter_copy(shard, n, i):
        hc = home_chip(shard, i)
        rel = (chip + nchip - hc) % nchip
        return send(
            dbuf.at[n, i],
            rsb.at[i // 2, rel - 1],
            rs_s.at[n, i],
            rs_r.at[i // 2, rel - 1],
            peer(hc),
        )

    def scatter(shard, n):
        got(sbuf.at[n], sr_r.at[n])
        for i in range(4):
            total = dbuf[n, i].astype(F32) + sbuf[n, i].astype(F32)
            at_home = home_chip(shard, i) == chip

            @pl.when(at_home)
            def _():
                own[i // 2] = total

            @pl.when(jnp.logical_not(at_home))
            def _():
                dbuf[n, i] = total.astype(BF)
                scatter_copy(shard, n, i).start()

    down(t, 0)
    scatter(t, 0)
    pending = [(t, 0)]
    n = 1
    done = 1
    for d in range(1, far + 1):
        for q in range(4):
            for v in range(2):
                if d == far and v != q // 2:
                    continue
                shard = (t + nz - d) % nz if v == 0 else (t + d) % nz
                got(hid.at[shard, pl.ds(q * unit, unit)], az_r.at[v, q, d - 1])
                if d < far - 1 or (d == far - 1 and v == q // 2):
                    cp = gather_copy(v, d, q)
                    cp.start()
                    waits.append(cp)
        todo = [(t + nz - d) % nz, (t + d) % nz] if d < far else [(t + far) % nz]
        for shard in todo:
            down(shard, n)
            pending.append((shard, n))
            n += 1
        for entry in pending[done:]:
            scatter(*entry)
        done = n

    for s in range(steps):
        total = own[s]
        for r in range(nchip - 1):
            got(rsb.at[s, r], rs_r.at[s, r])
            total = total + rsb[s, r].astype(F32)
        out_ref[s] = total.astype(BF)

    for cp in waits:
        cp.wait_send()
    for k in range(nz - 1):
        for q in range(2 * steps):
            for u in range(2):
                ring_copy(k, u, q).wait_send()
    for s in range(steps):

        for o in range(3):

            @pl.when(rel_z != near[o])
            def _():
                low_copy(s, o).wait_send()

        for i in range(3):

            @pl.when(kind == i)
            def _():
                for r in range(1, nchip):
                    low_out(s, i, r).wait_send()

    for shard, n in pending:
        for i in range(4):

            @pl.when(home_chip(shard, i) != chip)
            def _():
                scatter_copy(shard, n, i).wait_send()


def per_device(nx, ny, nz, act, wg, wu, wd, ws, we, scale, ids):
    steps, rows, feat = act.shape
    ff = wg.shape[1]
    dout = wd.shape[1]
    nrow = ids.shape[0]
    we = we.reshape(2, we.shape[1] * we.shape[2], ff)
    ids2 = ids.reshape(nrow // 128, 128)
    dma = pltpu.SemaphoreType.DMA
    nshard = 2 * nx
    chips = nx * ny
    nlow = chips * rows
    both = nrow * steps // nshard
    anyspec = pl.BlockSpec(memory_space=pl.ANY)
    vmem = pl.BlockSpec(memory_space=pltpu.VMEM)
    return pl.pallas_call(
        functools.partial(layer_kernel, nx, ny, nz),
        out_shape=jax.ShapeDtypeStruct((steps, rows, dout), BF),
        in_specs=[anyspec] * 6 + [pl.BlockSpec(memory_space=pltpu.SMEM), vmem],
        out_specs=vmem,
        scratch_shapes=[
            pltpu.VMEM((nshard, both, feat), BF),
            pltpu.VMEM(wg.shape, BF),
            pltpu.VMEM(wu.shape, BF),
            pltpu.VMEM(wd.shape, BF),
            pltpu.VMEM((ws.shape[0], 2 * ws.shape[1]), BF),
            pltpu.VMEM((2, 8, 128), F32),
            pltpu.VMEM(we.shape, BF),
            pltpu.VMEM((2, steps, nlow, 128), jnp.int32),
            pltpu.VMEM((steps, 128, nlow), BF),
            pltpu.VMEM((2, steps, nlow, 128), BF),
            pltpu.VMEM((2, 2, steps, nlow, 128), BF),
            pltpu.VMEM((2, steps, nlow, 256), BF),
            pltpu.VMEM((128, 256), BF),
            pltpu.VMEM((2, 128, 128), BF),
            pltpu.VMEM((steps, 2, 16, 128), BF),
            pltpu.VMEM((steps, nz - 1, 2, 16, 128), BF),
            pltpu.VMEM((steps, 3, 2, 2, 16, 128), BF),
            pltpu.VMEM((2, steps, 3, 2, 16, 128), BF),
            pltpu.VMEM((2, nshard, both, 256), BF),
            pltpu.VMEM((2, both, 256), BF),
            pltpu.VMEM(we.shape, BF),
            pltpu.VMEM((nz, both, ff), F32),
            pltpu.VMEM((nz, both, ff), F32),
            pltpu.VMEM((nz, both, ff), BF),
            pltpu.VMEM((nz, both, ff), BF),
            pltpu.VMEM((nz, both, ff), BF),
            pltpu.VMEM((nshard, 8, rows, dout), BF),
            pltpu.VMEM((nshard, 4, rows, dout), BF),
            pltpu.VMEM((steps, chips - 1, rows, dout), BF),
            pltpu.VMEM((steps, rows, dout), F32),
            dma((5,)),
            dma((steps,)),
            dma((steps, 3)),
            dma((steps, 3)),
            dma((steps, 4, 3)),
            dma((steps, 4, 3)),
            dma((steps,)),
            dma((steps,)),
            dma((2,)),
            dma((2,)),
            dma((steps, 3)),
            dma((steps, nz - 1)),
            dma((steps, chips - 1)),
            dma((steps, 3, 2)),
            dma((steps, 3)),
            dma((steps, 3)),
            dma((2,)),
            dma((2,)),
            dma((2, 2 * steps, nz - 1)),
            dma((2, 2 * steps, nz - 1)),
            dma((2, 4, 4)),
            dma((2, 4, 4)),
            dma((nshard,)),
            dma((nshard,)),
            dma((nshard, 4)),
            dma((steps, chips - 1)),
        ],
        compiler_params=pltpu.CompilerParams(
            collective_id=0, has_side_effects=True, vmem_limit_bytes=60 * 1024 * 1024
        ),
        name="layer",
    )(act, wg, wu, wd, ws, we, scale, ids2)


def solution(mesh):
    placed = (
        jax.sharding.PartitionSpec(None, "dp", "tensor"),
        jax.sharding.PartitionSpec("tensor", "dp"),
        jax.sharding.PartitionSpec("tensor", "dp"),
        jax.sharding.PartitionSpec("dp", "tensor"),
        jax.sharding.PartitionSpec("tensor", "dp"),
        jax.sharding.PartitionSpec(None, "tensor", None, "dp"),
        jax.sharding.PartitionSpec("dp"),
        jax.sharding.PartitionSpec(),
    )
    return jax.shard_map(
        functools.partial(per_device, 4, 4, mesh.shape["tensor"]),
        mesh=mesh,
        in_specs=placed,
        out_specs=jax.sharding.PartitionSpec(None, "dp", "tensor"),
        check_vma=False,
    )
```
